32 devices in a mesh: row: 4 (over x, core), col: 8 (over z, y).
Axes of the slice: x: 2, y: 2, z: 4, core: 2. Of those that a mesh axis runs over, the one named last changes fastest.
Arguments:
- cholesky: float32 [384, 896], P('row'), may hold values from -6 to 6
- denominators: float32 [384, 384], P('row', 'col'), may hold values from 10 to 40
- coupling: float32 [1], replicated, may hold values from 6 to 12
Outputs:
- amplitudes: float32 [384, 384], P('row', 'col')
The draws below stay inside these ranges and needn't reach their ends.
All inputs are finite; a program needn't handle non-finite values.
Results may differ from the reference program's by a relative error of at most 0.00013.
Values sent between devices are 32-bit elements; how exact they have to be, the bound alone decides.
A program may use at most 64 MiB of HBM per device.

```python
import jax
import jax.numpy as jnp
from jax import lax

CHOL = 896
ROUNDS = 2
INNER = 2
PAIRS = 384


def levels(key, extent, cuts, low, largest):
    def one(dim, shards_of):
        steps = jax.random.uniform(jax.random.fold_in(jax.random.fold_in(key, 6), dim), (shards_of,), jnp.float32, low / len(cuts), largest / len(cuts))
        return jnp.repeat(jnp.exp(steps), extent[dim] // shards_of).reshape((-1,) + (1,) * (len(extent) - dim - 1))

    level = one(*cuts[0])
    for cut in cuts[1:]:
        level = level * one(*cut)
    return level


def bell_draw(key, shape, width, limit, split=(), dtype=jnp.bfloat16):
    values = width * jax.random.normal(key, shape, jnp.float32)
    if split:
        values = values * levels(key, shape, split, -0.22, 0.18)
    return jnp.clip(values, -limit, limit).astype(dtype)


def setup_inputs(seed: int = 0) -> dict:
    seeds = jax.random.split(jax.random.key(seed), 4)
    return {
        "cholesky": bell_draw(seeds[0], (PAIRS, CHOL), 1.0, 6.0, ((0, 4),), jnp.float32),
        "denominators": jnp.clip(10.0 + 30.0 * jax.random.uniform(seeds[1], (PAIRS, PAIRS), jnp.float32) ** levels(seeds[1], (PAIRS, PAIRS), ((0, 4), (1, 8)), -0.2, 0.2), 10.0, 40.0),
        "coupling": jnp.clip(jax.random.uniform(seeds[2], (1,), jnp.float32, 6.0, 12.0), 6.0, 12.0),
    }


def reference(cholesky, denominators, coupling):
    highest = lax.Precision.HIGHEST
    strength = coupling[0] / PAIRS
    amplitudes = jnp.zeros((PAIRS, PAIRS), jnp.float32)
    started = False
    frozen = cholesky
    for round_index in range(ROUNDS):
        for step_index in range(INNER):
            if started:
                dressed = cholesky + strength * jnp.dot(amplitudes, cholesky, precision=highest, preferred_element_type=jnp.float32)
            else:
                dressed = cholesky
            if step_index == 0:
                frozen = dressed
            product = jnp.dot(dressed, frozen.T, precision=highest, preferred_element_type=jnp.float32)
            amplitudes = -product / denominators
            started = True
    return amplitudes
```

```python
import functools

import jax
import jax.numpy as jnp
from jax import lax
from jax.experimental import pallas as pl
from jax.experimental.pallas import tpu as pltpu
from jax.sharding import PartitionSpec as P

ROUNDS = 2
INNER = 2
LANES = 128
SUBLANES = 8
VMEM_BUDGET = 40 * 2**20
MESH = pl.DeviceIdType.MESH


precise = lax.Precision.HIGHEST


def broadcast(shard, axis, root):
    mine = lax.axis_index(axis) == root
    return lax.psum(jnp.where(mine, shard, jnp.zeros_like(shard)), axis)


def contract(left, right):
    return jnp.dot(left, right, precision=precise, preferred_element_type=jnp.float32)


def solve_tile(dressed, frozen, denominators):
    product = lax.dot_general(
        dressed,
        frozen,
        (((1,), (1,)), ((), ())),
        precision=precise,
        preferred_element_type=jnp.float32,
    )
    return -product / denominators


def refresh(dressed, within, block_cols, owner_row):
    return broadcast(lax.dynamic_slice_in_dim(dressed, within, block_cols, 0), "row", owner_row)


def distributed(cholesky, denominators, coupling):
    row_devices = lax.axis_size("row")
    col_devices = lax.axis_size("col")
    col_ratio = col_devices // row_devices
    block_rows = cholesky.shape[0]
    block_cols = denominators.shape[1]
    share_rows = block_rows // col_devices
    col_place = lax.axis_index("col")
    owner_row = col_place // col_ratio
    within = col_place % col_ratio * block_cols
    strength = coupling[0] / (block_rows * row_devices)
    chol_cols = broadcast(
        lax.dynamic_slice_in_dim(cholesky, within, block_cols, 0), "row", owner_row
    )
    own_rows = lax.dynamic_slice_in_dim(cholesky, col_place * share_rows, share_rows, 0)
    frozen = chol_cols
    amplitudes = solve_tile(cholesky, frozen, denominators)
    for round_index in range(ROUNDS):
        for step_index in range(INNER):
            if round_index == 0 and step_index == 0:
                continue
            row_piece = own_rows + strength * lax.psum_scatter(
                contract(amplitudes, chol_cols), "col", scatter_dimension=0, tiled=True
            )
            if step_index == 0:
                dressed = lax.all_gather(row_piece, "col", axis=0, tiled=True)
                frozen = refresh(dressed, within, block_cols, owner_row)
                amplitudes = solve_tile(dressed, frozen, denominators)
            else:
                amplitudes = solve_tile(
                    lax.all_gather(row_piece, "col", axis=0, tiled=True), frozen, denominators
                )
    return amplitudes


def halves(value):
    high = value.astype(jnp.bfloat16)
    low = (value - high.astype(jnp.float32)).astype(jnp.bfloat16)
    return high, low


def product(left, right, transposed):
    axis = 1 if transposed else 0
    wide = jnp.concatenate([left[0], left[1], left[0]], axis=1)
    deep = jnp.concatenate([right[0], right[0], right[1]], axis=axis)
    return lax.dot_general(
        wide, deep, (((1,), (axis,)), ((), ())), preferred_element_type=jnp.float32
    )


def gathered_kernel(
    rows_n, cols_n, coupling_ref, chol_ref, den_ref, out_ref,
    chol_all, den_all, flipped, inverse, gram, mixed,
    local_sem, send_sem, chol_sem, den_sem,
):
    block_rows, vectors = chol_ref.shape
    block_cols = den_ref.shape[0]
    pairs = block_rows * rows_n
    chunks = vectors // LANES
    over_y = chunks // 7
    over_x = chunks - over_y
    x_n, z_n = rows_n // 2, cols_n // 2
    row, col = lax.axis_index("row"), lax.axis_index("col")
    x, core = row // 2, row % 2
    z, y = col // 2, col % 2
    core_peer = (2 * x + 1 - core, col)
    y_peer = (row, 2 * z + 1 - y)
    x_away = [lax.rem(x + d, x_n) for d in range(1, x_n)]
    z_away = [lax.rem(z + d, z_n) for d in range(1, z_n)]
    x_peers = [(2 * far + core, col) for far in x_away]
    z_peers = [(row, 2 * far + y) for far in z_away]

    def rows_of(r):
        return pl.ds(pl.multiple_of(r * block_rows, SUBLANES), block_rows)

    def lanes_of(rel):
        start = rel + y * (chunks - 1 - 2 * rel)
        return pl.ds(pl.multiple_of(start * LANES, LANES), LANES)

    sent = []

    def send(src, dst, recv, peer):
        copy = pltpu.make_async_remote_copy(
            src_ref=src, dst_ref=dst, send_sem=send_sem.at[len(sent)], recv_sem=recv,
            device_id=peer, device_id_type=MESH,
        )
        copy.start()
        sent.append(copy)

    def arrived(ref, recv):
        pltpu.make_async_remote_copy(
            src_ref=ref, dst_ref=ref, send_sem=send_sem.at[0], recv_sem=recv,
            device_id=core_peer, device_id_type=MESH,
        ).wait_recv()

    def chol_at(r, rel):
        return chol_all.at[rows_of(r), lanes_of(rel)]

    def send_den(kc, ky, kz, kx, peer):
        block = den_all.at[kc, ky, kz, kx]
        send(block, block, den_sem.at[kc, ky, kz, kx], peer)

    def wait_den(kc, ky, kz, kx):
        arrived(den_all.at[kc, ky, kz, kx], den_sem.at[kc, ky, kz, kx])

    keep_den = pltpu.make_async_copy(den_ref, den_all.at[core, y, z, x], local_sem.at[0])
    keep_den.start()
    keep_chol = pltpu.make_async_copy(chol_ref, chol_all.at[rows_of(row), :], local_sem.at[1])
    keep_chol.start()
    peers = [core_peer, y_peer] + x_peers + z_peers
    barrier = pltpu.get_barrier_semaphore()
    for peer in peers:
        pl.semaphore_signal(barrier, inc=1, device_id=peer, device_id_type=MESH)
    pl.semaphore_wait(barrier, len(peers))

    def send_own(peer):
        send(den_ref, den_all.at[core, y, z, x], den_sem.at[core, y, z, x], peer)

    for peer in x_peers + z_peers:
        send_own(peer)
    for rel in range(over_x):
        for peer in x_peers:
            send(chol_ref.at[:, lanes_of(rel)], chol_at(row, rel), chol_sem.at[row, rel], peer)
    send_own(y_peer)
    send_own(core_peer)
    send(chol_ref, chol_all.at[rows_of(row), :], chol_sem.at[row, chunks], core_peer)
    for far in x_away:
        wait_den(core, y, z, far)
        for peer in z_peers + [y_peer, core_peer]:
            send_den(core, y, z, far, peer)

    def relay_chol(rel):
        for far in x_away:
            r = 2 * far + core
            arrived(chol_at(r, rel), chol_sem.at[r, rel])
            send(chol_at(r, rel), chol_at(r, rel), chol_sem.at[r, rel], core_peer)
            if rel < over_y:
                recv = chol_sem.at[r, chunks - 1 - rel]
                send(chol_at(r, rel), chol_at(r, rel), recv, y_peer)

    def accumulate(rel):
        if rel == 0:
            keep_chol.wait()
            other = core_peer[0]
            arrived(chol_all.at[rows_of(other), :], chol_sem.at[other, chunks])
        for far in x_away:
            r = 2 * far + 1 - core
            arrived(chol_at(r, rel), chol_sem.at[r, rel])
        split = halves(chol_all[:, lanes_of(rel)])
        term = product(split, split, True)
        if rel == 0:
            gram[...] = term
        else:
            gram[...] += term

    everywhere = [x] + x_away
    relays = [(y, kz, kx) for kz in z_away for kx in everywhere]
    onward = len(relays)
    relays += [(1 - y, kz, kx) for kz in [z] + z_away for kx in everywhere]
    per_step = -(-len(relays) // chunks)
    for rel in range(chunks):
        relay_chol(rel)
        for place in range(rel * per_step, min((rel + 1) * per_step, len(relays))):
            ky, kz, kx = relays[place]
            wait_den(core, ky, kz, kx)
            if place < onward:
                send_den(core, ky, kz, kx, y_peer)
            send_den(core, ky, kz, kx, core_peer)
        if rel >= 1:
            accumulate(rel - 1)
    accumulate(chunks - 1)
    keep_den.wait()
    for kz in [z] + z_away:
        for ky in (y, 1 - y):
            for kx in range(x_n):
                wait_den(1 - core, ky, kz, kx)
    for kx in range(x_n):
        for kc in range(2):
            r = 2 * kx + kc
            for c in range(cols_n):
                flipped[
                    c * block_cols : (c + 1) * block_cols, r * block_rows : (r + 1) * block_rows
                ] = 1.0 / den_all[kc, c % 2, c // 2, kx]
    inverse[...] = flipped[...].T

    strength = coupling_ref[0] * (1.0 / pairs)
    g = gram[...]
    g_split = halves(g)
    over = inverse[...]
    first = halves(-g * over)
    second = -(g + strength * product(first, g_split, False)) * over
    diagonal = lax.broadcasted_iota(jnp.int32, (pairs, pairs), 0) == lax.broadcasted_iota(
        jnp.int32, (pairs, pairs), 1
    )
    mixed[...] = jnp.where(diagonal, 1.0, 0.0) + strength * second
    m_split = halves(mixed[...])
    own_rows = pl.ds(pl.multiple_of(row * block_rows, SUBLANES), block_rows)
    own_cols = pl.ds(pl.multiple_of(col * block_cols, SUBLANES), block_cols)
    m_cols = mixed[own_cols, :]
    needed = jnp.concatenate([mixed[own_rows, :], m_cols], axis=0)
    dressed_gram = product(halves(needed), g_split, False)
    third = -product(halves(dressed_gram[:block_rows]), m_split, True) * inverse[own_rows, :]
    left = jnp.concatenate([gram[own_rows, :], strength * third], axis=1)
    right = jnp.concatenate([m_cols, dressed_gram[block_rows:]], axis=1)
    out_ref[...] = product(halves(right), halves(left), True)

    for copy in sent:
        copy.wait_send()


def gathered(rows_n, cols_n, cholesky, denominators, coupling):
    block_rows, vectors = cholesky.shape
    block_cols = denominators.shape[1]
    pairs = block_rows * rows_n
    x_n, z_n = rows_n // 2, cols_n // 2
    chunks = vectors // LANES
    sends = (x_n - 1) + (z_n - 1) + 2 + (x_n - 1) * (z_n + 1)
    sends += (x_n - 1) * 2 * chunks + 1 + x_n * (z_n - 1) * 2 + x_n * z_n
    vmem = pl.BlockSpec(memory_space=pltpu.VMEM)
    numerator = pl.pallas_call(
        functools.partial(gathered_kernel, rows_n, cols_n),
        out_shape=pltpu.VMEM((block_cols, block_rows), jnp.float32),
        in_specs=[pl.BlockSpec(memory_space=pltpu.SMEM), vmem, vmem],
        out_specs=vmem,
        scratch_shapes=[
            pltpu.VMEM((pairs, vectors), jnp.float32),
            pltpu.VMEM((2, 2, z_n, x_n, block_cols, block_rows), jnp.float32),
            pltpu.VMEM((pairs, pairs), jnp.float32),
            pltpu.VMEM((pairs, pairs), jnp.float32),
            pltpu.VMEM((pairs, pairs), jnp.float32),
            pltpu.VMEM((pairs, pairs), jnp.float32),
            pltpu.SemaphoreType.DMA((2,)),
            pltpu.SemaphoreType.DMA((sends,)),
            pltpu.SemaphoreType.DMA((rows_n, chunks + 1)),
            pltpu.SemaphoreType.DMA((2, 2, z_n, x_n)),
        ],
        compiler_params=pltpu.CompilerParams(collective_id=0, has_side_effects=True),
    )(coupling, cholesky, denominators.T)
    return -numerator.T / denominators


def fits(rows_n, cols_n, block_rows, block_cols, vectors):
    pairs = block_rows * rows_n
    regular = (
        rows_n % 2 == 0
        and cols_n % 2 == 0
        and vectors % LANES == 0
        and pairs % LANES == 0
        and block_rows % SUBLANES == 0
        and block_cols % SUBLANES == 0
        and block_rows <= LANES
        and vectors >= 4 * LANES
    )
    return regular and 4 * pairs * (vectors + 12 * pairs) <= VMEM_BUDGET


def per_device(rows_n, cols_n, cholesky, denominators, coupling):
    if fits(rows_n, cols_n, *denominators.shape, cholesky.shape[1]):
        return gathered(rows_n, cols_n, cholesky, denominators, coupling)
    return distributed(cholesky, denominators, coupling)


def solution(mesh):
    in_specs = (P("row", None), P("row", "col"), P())
    out_specs = P("row", "col")
    return jax.shard_map(
        functools.partial(per_device, mesh.shape["row"], mesh.shape["col"]),
        mesh=mesh, in_specs=in_specs, out_specs=out_specs, check_vma=False,
    )
```
